512 devices in a mesh: tm: 512 (over y, z, x, core).
Axes of the slice: x: 4, y: 4, z: 16, core: 2. Of those that a mesh axis runs over, the one named last changes fastest.
Arguments:
- trace: bfloat16 [262144, 512], P('tm'), may hold values from -6 to 6
- lengths: int32 [4], replicated, may hold values from 1 to 131072, as said below
- conv_weight: bfloat16 [2, 512, 1024], replicated, may hold values from -0.1875 to 0.1875
- res_weight: bfloat16 [512, 512], replicated, may hold values from -0.25 to 0.25
- cotangent: bfloat16 [262144, 512], P('tm'), may hold values from -6 to 6
Outputs:
- result: bfloat16 [262144, 512], P('tm')
- grad_input: bfloat16 [262144, 512], P('tm')
The draws below stay inside these ranges and needn't reach their ends.
Inputs may be any that keep to these rules, and one draw needn't show every extreme that they name: The 4 traces lie end to end from time 0 in this order and their lengths sum to 262144.
All inputs are finite; a program needn't handle non-finite values.
Results may differ from the reference program's by a relative error of at most 0.003.
Values may be sent and summed in bfloat16 or wider, within the bound.
No kernel may reach another device: no remote copies, remote signals or barrier semaphores. Data moves between devices by JAX's collectives and lax.ppermute only.
A program may use at most 64 MiB of HBM per device.

```python
import math
import jax
import jax.numpy as jnp
from jax import lax

RESIDUAL_WIDTH = 512
G = 512
T_DEV = 512
SAMPLE_COUNT = 262144
DILATION_STEP = 32768


def draw_lengths(key, part):
    first_key = jax.random.fold_in(key, 11)
    third_key = jax.random.fold_in(key, 23)
    first_end = jax.random.randint(first_key, (), SAMPLE_COUNT // 8, SAMPLE_COUNT // 4 + 1, dtype=jnp.int32)
    second_end = first_end + SAMPLE_COUNT // 2
    third_end = jax.random.randint(third_key, (), 3 * SAMPLE_COUNT // 4 + T_DEV, 7 * SAMPLE_COUNT // 8 - T_DEV + 1, dtype=jnp.int32)
    return jnp.stack([first_end, second_end - first_end, third_end - second_end, SAMPLE_COUNT - third_end]).astype(jnp.int32)


def level_of(stream_key, shape, pieces, smallest, high):
    def one(axis_at, blocks):
        heights = jax.random.uniform(jax.random.fold_in(jax.random.fold_in(stream_key, 6), axis_at), (blocks,), jnp.float32, smallest / len(pieces), high / len(pieces))
        return jnp.repeat(jnp.exp(heights), shape[axis_at] // blocks).reshape((-1,) + (1,) * (len(shape) - axis_at - 1))

    gain = one(*pieces[0])
    for cut in pieces[1:]:
        gain = gain * one(*cut)
    return gain


def noise(stream_key, dims, spread, most, shards=(), held_as=jnp.bfloat16):
    drawn = jax.random.normal(stream_key, dims, jnp.float32) * spread
    if len(shards) > 0:
        drawn = level_of(stream_key, dims, shards, -0.22, 0.18) * drawn
    return jnp.clip(drawn, min=-most, max=most).astype(held_as)


def setup_inputs(seed: int = 0) -> dict:
    splits = jax.random.split(jax.random.key(seed), 6)
    return {
        "trace": noise(splits[0], (SAMPLE_COUNT, RESIDUAL_WIDTH), 1.0, 6.0, ((0, 512),)),
        "lengths": draw_lengths(jax.random.fold_in(splits[5], 71), 0),
        "conv_weight": noise(splits[2], (2, RESIDUAL_WIDTH, 2 * G), (2 * RESIDUAL_WIDTH) ** -0.5, 0.1875),
        "res_weight": noise(splits[3], (G, RESIDUAL_WIDTH), G ** -0.5, 0.25),
        "cotangent": noise(splits[4], (SAMPLE_COUNT, RESIDUAL_WIDTH), 1.0, 6.0, ((0, 512),)),
    }


def reference(trace, lengths, conv_weight, res_weight, cotangent):
    sample_positions = jnp.arange(SAMPLE_COUNT, dtype=jnp.int32)
    row_starts = jnp.cumsum(lengths) - lengths
    total_len = jnp.sum(lengths)
    trace_begin = jnp.max(jnp.where(row_starts[None, :] <= sample_positions[:, None], row_starts[None, :], 0), axis=1)
    inside_trace = sample_positions < total_len
    delayed_mask = inside_trace & (sample_positions - DILATION_STEP >= trace_begin)
    delayed_rows = jnp.concatenate([jnp.zeros((DILATION_STEP, RESIDUAL_WIDTH), jnp.bfloat16), trace[:SAMPLE_COUNT - DILATION_STEP]], axis=0)
    delayed_rows = jnp.where(delayed_mask[:, None], delayed_rows, jnp.zeros_like(delayed_rows))
    block = math.gcd(SAMPLE_COUNT, 8192)
    count = SAMPLE_COUNT // block

    def one_block(args):
        now_rows, old_rows, cot_rows, valid_rows, tap_rows = args
        preact = jnp.dot(old_rows, conv_weight[0], preferred_element_type=jnp.float32)
        preact = preact + jnp.dot(now_rows, conv_weight[1], preferred_element_type=jnp.float32)
        filt_tanh = jnp.tanh(preact[:, :G])
        gate_sig = jax.nn.sigmoid(preact[:, G:])
        valid_f = valid_rows.astype(jnp.float32)[:, None]
        mixed = (filt_tanh * gate_sig * valid_f).astype(jnp.bfloat16)
        output = (now_rows.astype(jnp.float32) + jnp.dot(mixed, res_weight, preferred_element_type=jnp.float32)).astype(jnp.bfloat16)
        grad_mix = jnp.dot(cot_rows, res_weight.T, preferred_element_type=jnp.float32) * valid_f
        grad_filt = grad_mix * gate_sig * (1.0 - filt_tanh * filt_tanh)
        grad_gate = grad_mix * filt_tanh * gate_sig * (1.0 - gate_sig)
        grad_pre = jnp.concatenate([grad_filt, grad_gate], axis=1).astype(jnp.bfloat16)
        local_back = jnp.dot(grad_pre, conv_weight[1].T, preferred_element_type=jnp.float32)
        local_back = local_back + cot_rows.astype(jnp.float32)
        partial_output = jnp.dot(grad_pre, conv_weight[0].T, preferred_element_type=jnp.float32)
        partial_output = jnp.where(tap_rows[:, None], partial_output, 0.0).astype(jnp.bfloat16)
        return output, local_back, partial_output

    output, local_back, partial_output = lax.map(one_block, (
        trace.reshape(count, block, RESIDUAL_WIDTH), delayed_rows.reshape(count, block, RESIDUAL_WIDTH),
        cotangent.reshape(count, block, RESIDUAL_WIDTH), inside_trace.reshape(count, block), delayed_mask.reshape(count, block)))
    output = output.reshape(SAMPLE_COUNT, RESIDUAL_WIDTH)
    local_back = local_back.reshape(SAMPLE_COUNT, RESIDUAL_WIDTH)
    partial_output = partial_output.reshape(SAMPLE_COUNT, RESIDUAL_WIDTH)
    shifted_input = jnp.concatenate([partial_output[DILATION_STEP:], jnp.zeros((DILATION_STEP, RESIDUAL_WIDTH), jnp.bfloat16)], axis=0)
    grad_input = (local_back + shifted_input.astype(jnp.float32)).astype(jnp.bfloat16)
    return output, grad_input
```

```python
import jax
import jax.numpy as jnp
from jax import lax
from jax.sharding import PartitionSpec as P

CHUNKS = 2
CONTRACT = (((1,), (1,)), ((), ()))


def shift(value, axis, steps):
    count = lax.axis_size(axis)
    initial, last = (max(0, -steps), min(count, count - steps))
    return lax.ppermute(value, axis, [(source, source + steps) for source in range(initial, last)])


def per_device(trace, lengths, conv_weight, res_weight, cotangent):
    row_count = trace.shape[0]
    shard_gap = lax.axis_size("tm") // 8
    reach_rows = row_count * shard_gap
    half_width = conv_weight.shape[2] // 2
    size = row_count // CHUNKS
    parts = [slice(k * size, (k + 1) * size) for k in range(CHUNKS)]

    past = [shift(trace[part], "tm", shard_gap) for part in parts]

    positions = lax.axis_index("tm") * row_count + lax.broadcasted_iota(jnp.int32, (row_count, 1), 0)
    ends = [lengths[0]]
    for k in range(1, lengths.shape[0]):
        ends.append(ends[-1] + lengths[k])
    begin = jnp.zeros_like(positions)
    for k in range(lengths.shape[0] - 1):
        begin = jnp.where(ends[k] <= positions, jnp.maximum(begin, ends[k]), begin)
    inside = positions < ends[-1]
    tap = inside & (positions - reach_rows >= begin)
    valid = inside.astype(jnp.float32)

    here = jnp.dot(trace, conv_weight[1], preferred_element_type=jnp.float32)
    mix = lax.dot_general(cotangent, res_weight, CONTRACT, preferred_element_type=jnp.float32)

    outputs, locals_, partials = [], [], []
    for k, part in enumerate(parts):
        arrived, here_part, mix_part = past[k], here[part], mix[part]
        if k:
            arrived, here_part, mix_part, _ = lax.optimization_barrier(
                (arrived, here_part, mix_part, own)
            )
        delayed = jnp.where(tap[part], arrived, jnp.zeros_like(arrived))
        preact = jnp.dot(delayed, conv_weight[0], preferred_element_type=jnp.float32) + here_part
        filt_tanh = jnp.tanh(preact[:, :half_width])
        gate_sig = jax.nn.sigmoid(preact[:, half_width:])
        valid_f = valid[part]
        mixed = (filt_tanh * gate_sig * valid_f).astype(jnp.bfloat16)
        grad_mix = mix_part * valid_f
        grad_filt = grad_mix * gate_sig * (1.0 - filt_tanh * filt_tanh)
        grad_gate = grad_mix * filt_tanh * gate_sig * (1.0 - gate_sig)
        grad_pre = jnp.concatenate([grad_filt, grad_gate], axis=1).astype(jnp.bfloat16)
        own = lax.dot_general(grad_pre, conv_weight[0], CONTRACT, preferred_element_type=jnp.float32)
        own = jnp.where(tap[part], own, 0.0).astype(jnp.bfloat16)
        partials.append(shift(own, "tm", -shard_gap))
        outputs.append(
            (
                trace[part].astype(jnp.float32)
                + jnp.dot(mixed, res_weight, preferred_element_type=jnp.float32)
            ).astype(jnp.bfloat16)
        )
        back = lax.dot_general(grad_pre, conv_weight[1], CONTRACT, preferred_element_type=jnp.float32)
        locals_.append(cotangent[part].astype(jnp.float32) + back)
    grads = [
        (local + partial.astype(jnp.float32)).astype(jnp.bfloat16)
        for local, partial in zip(locals_, partials)
    ]
    return (jnp.concatenate(outputs, axis=0), jnp.concatenate(grads, axis=0))


def solution(mesh):
    in_specs = (P("tm", None), P(), P(), P(), P("tm", None))
    out_specs = (P("tm", None), P("tm", None))
    return jax.shard_map(
        per_device, mesh=mesh, in_specs=in_specs, out_specs=out_specs, check_vma=False
    )
```

```python
import functools

import jax
import jax.numpy as jnp
from jax import lax
from jax.experimental import pallas as pl
from jax.experimental.pallas import tpu as pltpu
from jax.sharding import PartitionSpec as P

BLOCKS = 8
CHUNKS = 2
CONTRACT = (((1,), (1,)), ((), ()))

ROUTES = (
    ((0, 2, 3, 4), ((4, 6), (3, 7)), ((0, 1), (2, 3)), ((6, 5), (7, 4))),
    ((0, 2, 3, 4, 6), ((3, 7),), ((0, 1), (2, 3), (4, 5), (6, 7)), ((7, 4),)),
    ((1, 2, 3, 5), ((2, 0), (3, 5), (5, 7)), ((1, 2),), ((0, 3), (5, 4), (7, 6))),
    ((1, 2, 3, 6), ((2, 0), (3, 5)), ((1, 2), (6, 7)), ((0, 3), (5, 4))),
    (tuple(range(BLOCKS - 1)), (), tuple((i, i + 1) for i in range(BLOCKS - 1)), ()),
)


def route_kernel(gap, rows, me_ref, lengths_ref, out_ref):
    position = lax.rem(me_ref[0], gap)
    reach = gap * rows
    starts = [lengths_ref[0]]
    for k in range(1, lengths_ref.shape[0] - 1):
        starts.append(starts[-1] + lengths_ref[k])
    total = starts[-1] + lengths_ref[lengths_ref.shape[0] - 1]
    live = []
    for edge in range(BLOCKS - 1):
        first = ((edge + 1) * gap + position) * rows
        dead = first >= total
        for start in starts:
            dead = dead | ((start <= first) & (first + rows <= start + reach))
        live.append(jnp.logical_not(dead))
    choice = jnp.int32(len(ROUTES) - 1)
    for k in reversed(range(len(ROUTES) - 1)):
        missed = jnp.bool_(False)
        for edge in range(BLOCKS - 1):
            if edge not in ROUTES[k][0]:
                missed = missed | live[edge]
        choice = jnp.where(missed, choice, jnp.int32(k))
    out_ref[0] = choice


def choose_route(me, lengths, gap, rows):
    smem = pl.BlockSpec(memory_space=pltpu.SMEM)
    return pl.pallas_call(
        functools.partial(route_kernel, gap, rows),
        out_shape=jax.ShapeDtypeStruct((1,), jnp.int32),
        in_specs=[smem, smem],
        out_specs=smem,
        name="route",
    )(me.reshape(1), lengths)[0]


def move(value, gap, hops):
    return lax.ppermute(
        value, "tm", [(a * gap + r, b * gap + r) for a, b in hops for r in range(gap)]
    )


def is_in(block, blocks):
    found = jnp.bool_(False)
    for b in blocks:
        found = found | (block == b)
    return found


def layer(route, gap, block, trace, conv_weight, res_weight, cotangent, tap, valid):
    edges, hops, own_sends, relay_sends = route
    returns = tuple((i + 1, i) for i in edges)
    row_count = trace.shape[0]
    half_width = conv_weight.shape[2] // 2
    size = row_count // CHUNKS
    parts = [slice(k * size, (k + 1) * size) for k in range(CHUNKS)]

    if hops:
        hopped = [move(trace[part], gap, hops) for part in parts]
    past = [move(trace[part], gap, own_sends) for part in parts]
    if hops:
        relayed = [move(value, gap, relay_sends) for value in hopped]
        by_relay = is_in(block, [b for _, b in relay_sends])
        past = [jnp.where(by_relay, b, a) for a, b in zip(past, relayed)]

    here = jnp.dot(trace, conv_weight[1], preferred_element_type=jnp.float32)
    mix = lax.dot_general(cotangent, res_weight, CONTRACT, preferred_element_type=jnp.float32)

    outputs, locals_, partials = [], [], []
    own = None
    for k, part in enumerate(parts):
        arrived, here_part, mix_part = past[k], here[part], mix[part]
        if k:
            arrived, here_part, mix_part, _ = lax.optimization_barrier(
                (arrived, here_part, mix_part, own)
            )
        delayed = jnp.where(tap[part], arrived, jnp.zeros_like(arrived))
        preact = jnp.dot(delayed, conv_weight[0], preferred_element_type=jnp.float32) + here_part
        filt_tanh = jnp.tanh(preact[:, :half_width])
        gate_sig = jax.nn.sigmoid(preact[:, half_width:])
        valid_f = valid[part]
        mixed = (filt_tanh * gate_sig * valid_f).astype(jnp.bfloat16)
        grad_mix = mix_part * valid_f
        grad_filt = grad_mix * gate_sig * (1.0 - filt_tanh * filt_tanh)
        grad_gate = grad_mix * filt_tanh * gate_sig * (1.0 - gate_sig)
        grad_pre = jnp.concatenate([grad_filt, grad_gate], axis=1).astype(jnp.bfloat16)
        own = lax.dot_general(grad_pre, conv_weight[0], CONTRACT, preferred_element_type=jnp.float32)
        own = jnp.where(tap[part], own, 0.0).astype(jnp.bfloat16)
        partials.append(move(own, gap, returns))
        outputs.append(
            (
                trace[part].astype(jnp.float32)
                + jnp.dot(mixed, res_weight, preferred_element_type=jnp.float32)
            ).astype(jnp.bfloat16)
        )
        back = lax.dot_general(grad_pre, conv_weight[1], CONTRACT, preferred_element_type=jnp.float32)
        locals_.append(cotangent[part].astype(jnp.float32) + back)
    grads = [
        (local + partial.astype(jnp.float32)).astype(jnp.bfloat16)
        for local, partial in zip(locals_, partials)
    ]
    return (jnp.concatenate(outputs, axis=0), jnp.concatenate(grads, axis=0))


def per_device(trace, lengths, conv_weight, res_weight, cotangent):
    row_count = trace.shape[0]
    gap = lax.axis_size("tm") // BLOCKS
    me = lax.axis_index("tm")
    choice = choose_route(me, lengths, gap, row_count)

    positions = me * row_count + lax.broadcasted_iota(jnp.int32, (row_count, 1), 0)
    ends = jnp.cumsum(lengths)
    starts = ends - lengths
    begin = jnp.max(jnp.where(starts[None, :] <= positions, starts[None, :], 0), axis=1, keepdims=True)
    inside = positions < jnp.sum(lengths)
    tap = inside & (positions - row_count * gap >= begin)
    valid = inside.astype(jnp.float32)

    branches = [functools.partial(layer, route, gap, me // gap) for route in ROUTES]
    return lax.switch(
        choice, branches, trace, conv_weight, res_weight, cotangent, tap, valid
    )


def solution(mesh):
    in_specs = (P("tm", None), P(), P(), P(), P("tm", None))
    out_specs = (P("tm", None), P("tm", None))
    return jax.shard_map(
        per_device, mesh=mesh, in_specs=in_specs, out_specs=out_specs, check_vma=False
    )
```

```python
import functools

import jax
import jax.numpy as jnp
from jax import lax
from jax.experimental import pallas as pl
from jax.experimental.pallas import tpu as pltpu
from jax.sharding import PartitionSpec as P


BLOCKS = 8
CONTRACT = (((1,), (1,)), ((), ()))


class Route:
    def __init__(self, edges, forward, backward):
        self.edges, self.forward, self.backward = edges, forward, backward


def plain(edges):
    forward = tuple((i, i + 1) for i in edges)
    backward = tuple((i + 1, i) for i in edges)
    return Route(tuple(edges), (forward, ()), (backward, ()))


def routed(forward, forward_splits, backward, backward_splits):
    edges = [a for a, _ in forward] + [a for a, _, _ in forward_splits]
    assert sorted(edges) == sorted([b for _, b in backward] + [b for _, _, b in backward_splits])
    return Route(tuple(edges), (forward, forward_splits), (backward, backward_splits))


ROUTES = (
    routed(
        ((2, 3), (4, 5)),
        ((0, 6, 1), (3, 7, 4)),
        ((1, 0), (5, 4)),
        ((3, 7, 2), (4, 6, 3)),
    ),
    routed(
        ((1, 2), (5, 6)),
        ((2, 0, 3), (3, 7, 4)),
        ((2, 1), (6, 5)),
        ((3, 7, 2), (4, 0, 3)),
    ),
    routed(
        ((1, 2), (6, 7)),
        ((2, 0, 3), (3, 5, 4)),
        ((2, 1), (7, 6)),
        ((3, 5, 2), (4, 0, 3)),
    ),
    plain((0, 2, 3, 4, 6)),
    plain(range(BLOCKS - 1)),
)


def route_kernel(gap, rows, me_ref, lengths_ref, out_ref):
    position = lax.rem(me_ref[0], gap)
    reach = gap * rows
    starts = [lengths_ref[0]]
    for k in range(1, lengths_ref.shape[0] - 1):
        starts.append(starts[-1] + lengths_ref[k])
    total = starts[-1] + lengths_ref[lengths_ref.shape[0] - 1]
    live = []
    for edge in range(BLOCKS - 1):
        first = ((edge + 1) * gap + position) * rows
        dead = first >= total
        for start in starts:
            dead = dead | ((start <= first) & (first + rows <= start + reach))
        live.append(jnp.logical_not(dead))
    choice = jnp.int32(len(ROUTES) - 1)
    for k in reversed(range(len(ROUTES) - 1)):
        missed = jnp.bool_(False)
        for edge in range(BLOCKS - 1):
            if edge not in ROUTES[k].edges:
                missed = missed | live[edge]
        choice = jnp.where(missed, choice, jnp.int32(k))
    out_ref[0] = choice


def choose_route(me, lengths, gap, rows):
    smem = pl.BlockSpec(memory_space=pltpu.SMEM)
    return pl.pallas_call(
        functools.partial(route_kernel, gap, rows),
        out_shape=jax.ShapeDtypeStruct((1,), jnp.int32),
        in_specs=[smem, smem],
        out_specs=smem,
        name="route",
    )(me.reshape(1), lengths)[0]


def move(value, gap, pairs):
    return lax.ppermute(
        value, "tm", [(a * gap + r, b * gap + r) for a, b in pairs for r in range(gap)]
    )


def among(block, blocks):
    found = block == blocks[0]
    for b in blocks[1:]:
        found = found | (block == b)
    return found


def exchange(first, second, gap, block, plan):
    sends, splits = plan
    if splits:
        held = move(second, gap, [(a, relay) for a, relay, _ in splits])
    first = move(first, gap, sends + tuple((a, b) for a, _, b in splits))
    second = move(second, gap, sends)
    if splits:
        passed = move(held, gap, [(relay, b) for _, relay, b in splits])
        second = jnp.where(among(block, [b for _, _, b in splits]), passed, second)
    return first, second


def layer(route, trace, me, lengths, conv_weight, res_weight, cotangent):
    row_count = trace.shape[0]
    half = row_count // 2
    gap = lax.axis_size("tm") // BLOCKS
    block = lax.div(me, jnp.int32(gap))
    half_width = conv_weight.shape[2] // 2

    past = exchange(trace[:half], trace[half:], gap, block, route.forward)

    positions = me * row_count + lax.broadcasted_iota(jnp.int32, (row_count, 1), 0)
    ends = jnp.cumsum(lengths)
    starts = ends - lengths
    begin = jnp.max(jnp.where(starts[None, :] <= positions, starts[None, :], 0), axis=1, keepdims=True)
    inside = positions < jnp.sum(lengths)
    tap = inside & (positions - row_count * gap >= begin)
    valid_f = inside.astype(jnp.float32)

    delayed = jnp.where(tap, jnp.concatenate(past, axis=0), jnp.bfloat16(0))
    taps = jnp.concatenate([delayed, trace], axis=1)
    preact = jnp.dot(
        taps, conv_weight.reshape(-1, conv_weight.shape[2]), preferred_element_type=jnp.float32
    )
    filt_tanh = jnp.tanh(preact[:, :half_width])
    gate_sig = jax.nn.sigmoid(preact[:, half_width:])
    mixed = (filt_tanh * gate_sig * valid_f).astype(jnp.bfloat16)
    mix = lax.dot_general(cotangent, res_weight, CONTRACT, preferred_element_type=jnp.float32)
    grad_mix = mix * valid_f
    grad_filt = grad_mix * gate_sig * (1.0 - filt_tanh * filt_tanh)
    grad_gate = grad_mix * filt_tanh * gate_sig * (1.0 - gate_sig)
    grad_pre = jnp.concatenate([grad_filt, grad_gate], axis=1).astype(jnp.bfloat16)

    def own(rows):
        value = lax.dot_general(
            grad_pre[rows], conv_weight[0], CONTRACT, preferred_element_type=jnp.float32
        )
        return jnp.where(tap[rows], value, 0.0).astype(jnp.bfloat16)

    own_first, own_second = own(slice(0, half)), own(slice(half, row_count))
    partial = exchange(own_first, own_second, gap, block, route.backward)
    output = (
        trace.astype(jnp.float32) + jnp.dot(mixed, res_weight, preferred_element_type=jnp.float32)
    ).astype(jnp.bfloat16)
    local = cotangent.astype(jnp.float32) + lax.dot_general(
        grad_pre, conv_weight[1], CONTRACT, preferred_element_type=jnp.float32
    )
    local = lax.optimization_barrier(local)
    partial = jnp.concatenate(partial, axis=0).astype(jnp.float32)
    return (output, (local + partial).astype(jnp.bfloat16))


def per_device(trace, lengths, conv_weight, res_weight, cotangent):
    gap = lax.axis_size("tm") // BLOCKS
    me = lax.axis_index("tm")
    choice = choose_route(me, lengths, gap, trace.shape[0])
    branches = [functools.partial(layer, route) for route in ROUTES]
    return lax.switch(choice, branches, trace, me, lengths, conv_weight, res_weight, cotangent)


def solution(mesh):
    in_specs = (P("tm", None), P(), P(), P(), P("tm", None))
    out_specs = (P("tm", None), P("tm", None))
    return jax.shard_map(
        per_device, mesh=mesh, in_specs=in_specs, out_specs=out_specs, check_vma=False
    )
```

```python
import functools

import jax
import jax.numpy as jnp
from jax import lax
from jax.experimental import pallas as pl
from jax.experimental.pallas import tpu as pltpu
from jax.sharding import PartitionSpec as P


BLOCKS = 8
CONTRACT = (((1,), (1,)), ((), ()))

VARIANTS = 3
SLICES = 4


class Route:
    def __init__(self, edges, forward, backward):
        self.edges, self.forward, self.backward = edges, forward, backward


def plain(edges):
    forward = ((tuple((i, i + 1) for i in edges), ()),)
    backward = tuple(
        (tuple((i + 1, i) for i in edges if i % 2 == odd), ()) for odd in range(2)
    )
    return Route(tuple(edges), (forward,) * VARIANTS, (backward,) * VARIANTS)


def group(sends, relays):
    return (
        tuple((a, b) for a, b in sends if a not in relays),
        tuple((a, relays[a], b) for a, b in sends if a in relays),
    )


def routed(many, lone, relays, back_relays):
    forward = [(group([(i, i + 1) for i in sorted(many + lone)], r),) for r in relays]
    backward = [
        tuple(group([(i + 1, i) for i in edges], r) for edges in (many, lone)) for r in back_relays
    ]
    return Route(many + lone, forward, backward)


ROUTES = (
    routed(
        (0, 2, 4),
        (3,),
        [{a: 6, 3: 7} for a in (0, 2, 4)],
        [{a: 7, 4: 6} for a in (1, 3, 5)],
    ),
    routed(
        (1, 3, 5),
        (2,),
        [{a: 7, 2: 0} for a in (1, 3, 5)],
        [{a: 0, 3: 7} for a in (2, 4, 6)],
    ),
    routed(
        (1, 3),
        (2, 6),
        [{a: 5, 2: 0} for a in (1, 3, 1)],
        [{a: 0, 3: 5} for a in (4, 2, 4)],
    ),
    plain((0, 2, 3, 4, 6)),
    plain(range(BLOCKS - 1)),
)


def route_kernel(gap, rows, me_ref, lengths_ref, out_ref):
    position = lax.rem(me_ref[0], gap)
    reach = gap * rows
    starts = [lengths_ref[0]]
    for k in range(1, lengths_ref.shape[0] - 1):
        starts.append(starts[-1] + lengths_ref[k])
    total = starts[-1] + lengths_ref[lengths_ref.shape[0] - 1]
    live = []
    for edge in range(BLOCKS - 1):
        first = ((edge + 1) * gap + position) * rows
        dead = first >= total
        for start in starts:
            dead = dead | ((start <= first) & (first + rows <= start + reach))
        live.append(jnp.logical_not(dead))
    choice = jnp.int32(len(ROUTES) - 1)
    for k in reversed(range(len(ROUTES) - 1)):
        missed = jnp.bool_(False)
        for edge in range(BLOCKS - 1):
            if edge not in ROUTES[k].edges:
                missed = missed | live[edge]
        choice = jnp.where(missed, choice, jnp.int32(k))
    out_ref[0] = choice


def choose_route(me, lengths, gap, rows):
    smem = pl.BlockSpec(memory_space=pltpu.SMEM)
    return pl.pallas_call(
        functools.partial(route_kernel, gap, rows),
        out_shape=jax.ShapeDtypeStruct((1,), jnp.int32),
        in_specs=[smem, smem],
        out_specs=smem,
        name="route",
    )(me.reshape(1), lengths)[0]


def move(value, gap, pairs):
    width = gap // SLICES
    return lax.ppermute(
        value,
        "tm",
        [
            (a * gap + r, b * gap + r)
            for r in range(gap)
            for a, b in pairs[(r // width) % VARIANTS]
        ],
    )


def among(place, blocks):
    block, variant = place
    if all(set(b) == set(blocks[0]) for b in blocks):
        blocks, variant = blocks[:1], None
    found = jnp.bool_(False)
    for v, names in enumerate(blocks):
        here = jnp.bool_(False)
        for b in names:
            here = here | (block == b)
        found = found | (here if variant is None else here & (variant == v))
    return found


def exchange(first, second, gap, place, plans):
    splits = [[split for group in plan for split in group[1]] for plan in plans]
    if splits[0]:
        held = move(second, gap, [[(a, relay) for a, relay, _ in s] for s in splits])
    near = next_ = None
    for k in range(len(plans[0])):
        sends = [plan[k][0] for plan in plans]
        direct = [plan[k][0] + tuple((a, b) for a, _, b in plan[k][1]) for plan in plans]
        arrived = move(first, gap, direct)
        here = among(place, [[b for _, b in d] for d in direct])
        near = arrived if near is None else jnp.where(here, arrived, near)
        if sends[0]:
            arrived = move(second, gap, sends)
            next_ = arrived if next_ is None else jnp.where(here, arrived, next_)
    if splits[0]:
        passed = move(held, gap, [[(relay, b) for _, relay, b in s] for s in splits])
        next_ = jnp.where(among(place, [[b for _, _, b in s] for s in splits]), passed, next_)
    return near, next_


def layer(route, trace, me, lengths, conv_weight, res_weight, cotangent):
    row_count = trace.shape[0]
    half = row_count // 2
    gap = lax.axis_size("tm") // BLOCKS
    block = lax.div(me, jnp.int32(gap))
    variant = lax.rem(lax.div(lax.rem(me, jnp.int32(gap)), jnp.int32(gap // SLICES)), jnp.int32(VARIANTS))
    place = (block, variant)
    half_width = conv_weight.shape[2] // 2

    past = exchange(trace[:half], trace[half:], gap, place, route.forward)
    here = jnp.dot(trace, conv_weight[1], preferred_element_type=jnp.float32)

    positions = me * row_count + lax.broadcasted_iota(jnp.int32, (row_count, 1), 0)
    ends = jnp.cumsum(lengths)
    starts = ends - lengths
    begin = jnp.max(jnp.where(starts[None, :] <= positions, starts[None, :], 0), axis=1, keepdims=True)
    inside = positions < jnp.sum(lengths)
    tap = inside & (positions - row_count * gap >= begin)
    valid_f = inside.astype(jnp.float32)

    delayed = jnp.where(tap, jnp.concatenate(past, axis=0), jnp.bfloat16(0))
    delayed = lax.optimization_barrier(delayed)
    preact = jnp.dot(delayed, conv_weight[0], preferred_element_type=jnp.float32) + here
    filt_tanh = jnp.tanh(preact[:, :half_width])
    gate_sig = jax.nn.sigmoid(preact[:, half_width:])
    mixed = (filt_tanh * gate_sig * valid_f).astype(jnp.bfloat16)
    mix = lax.dot_general(cotangent, res_weight, CONTRACT, preferred_element_type=jnp.float32)
    grad_mix = mix * valid_f
    grad_filt = grad_mix * gate_sig * (1.0 - filt_tanh * filt_tanh)
    grad_gate = grad_mix * filt_tanh * gate_sig * (1.0 - gate_sig)
    grad_pre = jnp.concatenate([grad_filt, grad_gate], axis=1).astype(jnp.bfloat16)

    def own(rows):
        value = lax.dot_general(
            grad_pre[rows], conv_weight[0], CONTRACT, preferred_element_type=jnp.float32
        )
        return jnp.where(tap[rows], value, 0.0).astype(jnp.bfloat16)

    own_first, own_second = own(slice(0, half)), own(slice(half, row_count))
    partial = exchange(own_first, own_second, gap, place, route.backward)
    output = (
        trace.astype(jnp.float32) + jnp.dot(mixed, res_weight, preferred_element_type=jnp.float32)
    ).astype(jnp.bfloat16)
    local = cotangent.astype(jnp.float32) + lax.dot_general(
        grad_pre, conv_weight[1], CONTRACT, preferred_element_type=jnp.float32
    )
    local = lax.optimization_barrier(local)
    partial = jnp.concatenate(partial, axis=0).astype(jnp.float32)
    return (output, (local + partial).astype(jnp.bfloat16))


def per_device(trace, lengths, conv_weight, res_weight, cotangent):
    gap = lax.axis_size("tm") // BLOCKS
    me = lax.axis_index("tm")
    choice = choose_route(me, lengths, gap, trace.shape[0])
    branches = [functools.partial(layer, route) for route in ROUTES]
    return lax.switch(choice, branches, trace, me, lengths, conv_weight, res_weight, cotangent)


def solution(mesh):
    in_specs = (P("tm", None), P(), P(), P(), P("tm", None))
    out_specs = (P("tm", None), P("tm", None))
    return jax.shard_map(
        per_device, mesh=mesh, in_specs=in_specs, out_specs=out_specs, check_vma=False
    )
```

```python
import functools

import jax
import jax.numpy as jnp
from jax import lax
from jax.experimental import pallas as pl
from jax.experimental.pallas import tpu as pltpu
from jax.sharding import PartitionSpec as P


BLOCKS = 8
CONTRACT = (((1,), (1,)), ((), ()))

VARIANTS = 3
SLICES = 4


class Route:
    def __init__(self, edges, forward, backward):
        self.edges, self.forward, self.backward = edges, forward, backward


def plain(edges):
    forward = ((tuple((i, i + 1) for i in edges), ()),)
    backward = tuple(
        (tuple((i + 1, i) for i in edges if i % 2 == odd), ()) for odd in range(2)
    )
    return Route(tuple(edges), (forward,) * VARIANTS, (backward,) * VARIANTS)


def group(sends, relays):
    return (
        tuple((a, b) for a, b in sends if a not in relays),
        tuple((a, relays[a], b) for a, b in sends if a in relays),
    )


def routed(many, lone, relays, back_relays):
    forward = [(group([(i, i + 1) for i in sorted(many + lone)], r),) for r in relays]
    backward = [
        tuple(group([(i + 1, i) for i in edges], r) for edges in (many, lone)) for r in back_relays
    ]
    return Route(many + lone, forward, backward)


ROUTES = (
    routed(
        (0, 2, 4),
        (3,),
        [{a: 6, 3: 7} for a in (0, 2, 4)],
        [{a: 7, 4: 6} for a in (1, 3, 5)],
    ),
    routed(
        (1, 3, 5),
        (2,),
        [{a: 7, 2: 0} for a in (1, 3, 5)],
        [{a: 0, 3: 7} for a in (2, 4, 6)],
    ),
    routed(
        (1, 3),
        (2, 6),
        [{a: 5, 2: 0, 6: 4} for a in (1, 3, 1)],
        [{a: 0, 3: 5, 7: 1} for a in (4, 2, 4)],
    ),
    plain((0, 2, 3, 4, 6)),
    plain(range(BLOCKS - 1)),
)


def route_kernel(gap, rows, me_ref, lengths_ref, out_ref):
    position = lax.rem(me_ref[0], gap)
    reach = gap * rows
    starts = [lengths_ref[0]]
    for k in range(1, lengths_ref.shape[0] - 1):
        starts.append(starts[-1] + lengths_ref[k])
    total = starts[-1] + lengths_ref[lengths_ref.shape[0] - 1]
    live = []
    for edge in range(BLOCKS - 1):
        first = ((edge + 1) * gap + position) * rows
        dead = first >= total
        for start in starts:
            dead = dead | ((start <= first) & (first + rows <= start + reach))
        live.append(jnp.logical_not(dead))
    choice = jnp.int32(len(ROUTES) - 1)
    for k in reversed(range(len(ROUTES) - 1)):
        missed = jnp.bool_(False)
        for edge in range(BLOCKS - 1):
            if edge not in ROUTES[k].edges:
                missed = missed | live[edge]
        choice = jnp.where(missed, choice, jnp.int32(k))
    out_ref[0] = choice


def choose_route(me, lengths, gap, rows):
    smem = pl.BlockSpec(memory_space=pltpu.SMEM)
    return pl.pallas_call(
        functools.partial(route_kernel, gap, rows),
        out_shape=jax.ShapeDtypeStruct((1,), jnp.int32),
        in_specs=[smem, smem],
        out_specs=smem,
        name="route",
    )(me.reshape(1), lengths)[0]


def move(value, gap, pairs):
    width = gap // SLICES
    return lax.ppermute(
        value,
        "tm",
        [
            (a * gap + r, b * gap + r)
            for r in range(gap)
            for a, b in pairs[(r // width) % VARIANTS]
        ],
    )


def among(place, blocks):
    block, variant = place
    if all(set(b) == set(blocks[0]) for b in blocks):
        blocks, variant = blocks[:1], None
    found = jnp.bool_(False)
    for v, names in enumerate(blocks):
        here = jnp.bool_(False)
        for b in names:
            here = here | (block == b)
        found = found | (here if variant is None else here & (variant == v))
    return found


def send_near(first, gap, place, plans):
    near = None
    for k in range(len(plans[0])):
        direct = [plan[k][0] + tuple((a, b) for a, _, b in plan[k][1]) for plan in plans]
        arrived = move(first, gap, direct)
        here = among(place, [[b for _, b in d] for d in direct])
        near = arrived if near is None else jnp.where(here, arrived, near)
    return near


def send_rest(second, gap, place, plans):
    splits = [[split for group in plan for split in group[1]] for plan in plans]
    if splits[0]:
        held = move(second, gap, [[(a, relay) for a, relay, _ in s] for s in splits])
    next_ = None
    for k in range(len(plans[0])):
        sends = [plan[k][0] for plan in plans]
        if sends[0]:
            arrived = move(second, gap, sends)
            here = among(place, [[b for _, b in s] for s in sends])
            next_ = arrived if next_ is None else jnp.where(here, arrived, next_)
    if splits[0]:
        passed = move(held, gap, [[(relay, b) for _, relay, b in s] for s in splits])
        next_ = jnp.where(among(place, [[b for _, _, b in s] for s in splits]), passed, next_)
    return next_


def layer(route, trace, me, lengths, conv_weight, res_weight, cotangent):
    row_count = trace.shape[0]
    half = row_count // 2
    gap = lax.axis_size("tm") // BLOCKS
    block = lax.div(me, jnp.int32(gap))
    variant = lax.rem(lax.div(lax.rem(me, jnp.int32(gap)), jnp.int32(gap // SLICES)), jnp.int32(VARIANTS))
    place = (block, variant)
    half_width = conv_weight.shape[2] // 2

    near = send_near(trace[:half], gap, place, route.forward)
    rest = send_rest(trace[half:], gap, place, route.forward)
    here = jnp.dot(trace, conv_weight[1], preferred_element_type=jnp.float32)

    positions = me * row_count + lax.broadcasted_iota(jnp.int32, (row_count, 1), 0)
    ends = jnp.cumsum(lengths)
    starts = ends - lengths
    begin = jnp.max(jnp.where(starts[None, :] <= positions, starts[None, :], 0), axis=1, keepdims=True)
    inside = positions < jnp.sum(lengths)
    tap = inside & (positions - row_count * gap >= begin)
    valid_f = inside.astype(jnp.float32)

    def compute(rows, past):
        delayed = lax.optimization_barrier(jnp.where(tap[rows], past, jnp.bfloat16(0)))
        preact = jnp.dot(delayed, conv_weight[0], preferred_element_type=jnp.float32) + here[rows]
        filt_tanh = jnp.tanh(preact[:, :half_width])
        gate_sig = jax.nn.sigmoid(preact[:, half_width:])
        mixed = (filt_tanh * gate_sig * valid_f[rows]).astype(jnp.bfloat16)
        mix = lax.dot_general(
            cotangent[rows], res_weight, CONTRACT, preferred_element_type=jnp.float32
        )
        grad_mix = mix * valid_f[rows]
        grad_filt = grad_mix * gate_sig * (1.0 - filt_tanh * filt_tanh)
        grad_gate = grad_mix * filt_tanh * gate_sig * (1.0 - gate_sig)
        grad_pre = jnp.concatenate([grad_filt, grad_gate], axis=1).astype(jnp.bfloat16)
        own = lax.dot_general(
            grad_pre, conv_weight[0], CONTRACT, preferred_element_type=jnp.float32
        )
        own = jnp.where(tap[rows], own, 0.0).astype(jnp.bfloat16)
        return own, grad_pre, mixed

    own_first, grad_first, mixed_first = compute(slice(0, half), near)
    rest, _ = lax.optimization_barrier((rest, own_first))
    own_second, grad_second, mixed_second = compute(slice(half, row_count), rest)
    partial = (
        send_near(own_first, gap, place, route.backward),
        send_rest(own_second, gap, place, route.backward),
    )
    grad_pre = jnp.concatenate([grad_first, grad_second], axis=0)
    mixed = jnp.concatenate([mixed_first, mixed_second], axis=0)
    output = (
        trace.astype(jnp.float32) + jnp.dot(mixed, res_weight, preferred_element_type=jnp.float32)
    ).astype(jnp.bfloat16)
    local = cotangent.astype(jnp.float32) + lax.dot_general(
        grad_pre, conv_weight[1], CONTRACT, preferred_element_type=jnp.float32
    )
    local = lax.optimization_barrier(local)
    partial = jnp.concatenate(partial, axis=0).astype(jnp.float32)
    return (output, (local + partial).astype(jnp.bfloat16))


def per_device(trace, lengths, conv_weight, res_weight, cotangent):
    gap = lax.axis_size("tm") // BLOCKS
    me = lax.axis_index("tm")
    choice = choose_route(me, lengths, gap, trace.shape[0])
    branches = [functools.partial(layer, route) for route in ROUTES]
    return lax.switch(choice, branches, trace, me, lengths, conv_weight, res_weight, cotangent)


def solution(mesh):
    in_specs = (P("tm", None), P(), P(), P(), P("tm", None))
    out_specs = (P("tm", None), P("tm", None))
    return jax.shard_map(
        per_device, mesh=mesh, in_specs=in_specs, out_specs=out_specs, check_vma=False
    )
```
